768 devices in a mesh: group: 4 (over y_lo), blk: 48 (over y_hi, z, core), mp: 4 (over x).
Axes of the slice: x: 4, y: 8 (y_hi: 2, y_lo: 4; y = y_hi * 4 + y_lo), z: 12, core: 2. Of those that a mesh axis runs over, the one named last changes fastest.
Arguments:
- image_hidden: bfloat16 [12288, 1408], P('blk', 'mp'), may hold values from -6 to 6
- image_weight: bfloat16 [1408, 1536], P('mp'), may hold values from -0.00390625 to 0.00390625
- text_embed: bfloat16 [12288, 1536], P(('group', 'blk', 'mp')), may hold values from -0.19921875 to 0.19921875
- positives: int32 [12288], P('blk'), may hold values from 0 to 12287, each once
- log_temp: float32 [1], replicated, may hold values from 1.6 to 3
- bias: float32 [1], replicated, may hold values from -10 to -5
Outputs:
- loss: float32 [1], replicated
- grad_temp: float32 [1], replicated
- grad_bias: float32 [1], replicated
- grad_image: float32 [12288, 1536], P('blk')
- grad_text: float32 [12288, 1536], P(('group', 'blk', 'mp'))
- grad_weight: float32 [1408, 1536], P('mp', ('group', 'blk'))
The draws below stay inside these ranges and needn't reach their ends.
Inputs may be any that keep to these rules, and one draw needn't show every extreme that they name: positives is a permutation: every text is the positive of exactly one image.
All inputs are finite; a program needn't handle non-finite values.
Results may differ from the reference program's by a relative error of at most 0.0045.
Values may be sent and summed in bfloat16 or wider, within the bound.
No kernel may reach another device: no remote copies, remote signals or barrier semaphores. Data moves between devices by JAX's collectives and lax.ppermute only.
A program may use at most 32 MiB of HBM per device.

```python
import jax
import jax.numpy as jnp
from jax import lax

H = 1408
E = 1536
PAIRS = 12288


def steps_of(key, dims, pieces, least, top_value):
    level = 1.0
    for dim, shards_of in pieces:
        steps = jax.random.uniform(jax.random.fold_in(jax.random.fold_in(key, 6), dim), (shards_of,), jnp.float32, least / len(pieces), top_value / len(pieces))
        level = level * jnp.repeat(jnp.exp(steps), dims[dim] // shards_of).reshape((-1,) + (1,) * (len(dims) - 1 - dim))
    return level


def gaussian(own_key, dims, scale, most, cuts=(), kind=jnp.bfloat16):
    entries = scale * jax.random.normal(own_key, dims, jnp.float32)
    if cuts:
        entries = entries * steps_of(own_key, dims, cuts, -0.22, 0.18)
    return jnp.clip(entries, -most, most).astype(kind)


def setup_inputs(seed: int = 0) -> dict:
    keys = jax.random.split(jax.random.key(seed), 7)
    image_hidden = gaussian(keys[0], (PAIRS, H), 1.0, 6.0, ((0, 48), (1, 4)))
    image_weight = gaussian(keys[1], (H, E), (H * E) ** -0.5, 0.00390625, ((0, 4),))
    text_embed = gaussian(keys[2], (PAIRS, E), 0.03, 0.19921875, ((0, 768),))
    positives = jax.random.permutation(keys[3], PAIRS).astype(jnp.int32)
    log_temp = jnp.clip(jax.random.uniform(keys[4], (1,), jnp.float32, 1.6, 3.0), 1.6, 3.0)
    bias = jnp.clip(jax.random.uniform(keys[5], (1,), jnp.float32, -10.0, -5.0), -10.0, -5.0)
    return dict(image_hidden=image_hidden, image_weight=image_weight, text_embed=text_embed, positives=positives, log_temp=log_temp, bias=bias)


def unit_rows(values):
    norm_rows = jnp.sqrt(lax.optimization_barrier(jnp.sum(values * values, axis=1, keepdims=True)) + 1e-06)
    return (values / norm_rows, norm_rows)

def unit_backward(grads, unit, norm_rows):
    return (grads - unit * lax.optimization_barrier(jnp.sum(unit * grads, axis=1, keepdims=True))) / norm_rows

def reference(image_hidden, image_weight, text_embed, positives, log_temp, bias):
    image_emb = jnp.dot(image_hidden, image_weight, preferred_element_type=jnp.float32)
    image_unit, image_norm = unit_rows(image_emb)
    image_low = image_unit.astype(jnp.bfloat16)
    text_unit, text_norm = unit_rows(text_embed.astype(jnp.float32))
    text_low = text_unit.astype(jnp.bfloat16)
    scale = jnp.exp(log_temp[0])
    sims = jnp.dot(image_low, text_low.T, preferred_element_type=jnp.float32)
    logits = scale * sims + bias[0]
    column = jnp.arange(PAIRS, dtype=jnp.int32)
    signs = jnp.where(column[None, :] == positives[:, None], 1.0, -1.0).astype(jnp.float32)
    loss = -jnp.sum(jax.nn.log_sigmoid(signs * logits)) / PAIRS
    slopes = -signs * jax.nn.sigmoid(-signs * logits)
    grad_temp = scale * jnp.sum(slopes * sims) / PAIRS
    grad_bias = jnp.sum(slopes) / PAIRS
    weights = (scale * slopes).astype(jnp.bfloat16)
    grad_unit_image = jnp.dot(weights, text_low, preferred_element_type=jnp.float32)
    grad_unit_text = jnp.dot(weights.T, image_low, preferred_element_type=jnp.float32)
    grad_image = unit_backward(grad_unit_image, image_unit, image_norm)
    grad_text = unit_backward(grad_unit_text, text_unit, text_norm)
    grad_weight = jnp.dot(image_hidden.T, grad_image.astype(jnp.bfloat16), preferred_element_type=jnp.float32)
    return (loss.reshape(1), grad_temp.reshape(1), grad_bias.reshape(1), grad_image, grad_text, grad_weight)
```

```python
import jax
import jax.numpy as jnp
from jax import lax
from jax.sharding import Mesh
from jax.sharding import PartitionSpec as P

F32 = jnp.float32
BF16 = jnp.bfloat16


def unit_rows(values):
    norm_rows = jnp.sqrt(jnp.sum(values * values, axis=1, keepdims=True) + 1e-06)
    return (values / norm_rows, norm_rows)


def unit_backward(grads, unit, norm_rows):
    return (grads - unit * jnp.sum(unit * grads, axis=1, keepdims=True)) / norm_rows


def swap(values, axis):
    return lax.ppermute(values, axis, [(0, 1), (1, 0)])


def on_device(image_hidden, image_weight, text_embed, positives, log_temp, bias):
    groups = lax.axis_size("group")
    halves = lax.axis_size("yh")
    rings = lax.axis_size("z")
    cores = lax.axis_size("core")
    splits = lax.axis_size("mp")
    group_id = lax.axis_index("group")
    half = lax.axis_index("yh")
    core = lax.axis_index("core")
    share = lax.axis_index("mp")
    rows = image_hidden.shape[0]
    blocks = halves * rings * cores
    pairs = rows * blocks
    width = text_embed.shape[0]
    embed = text_embed.shape[1]
    hidden = image_hidden.shape[1]

    text_unit, text_norm = unit_rows(text_embed.astype(F32))
    text_low = text_unit.astype(BF16)
    two = lax.all_gather(text_low, "yh", axis=0, tiled=True)
    piece = lax.all_gather(two, "z", axis=0, tiled=True)
    count = piece.shape[0]

    partial_value = jnp.dot(image_hidden, image_weight, preferred_element_type=F32)
    parts = lax.all_to_all(partial_value, "mp", 0, 0, tiled=True)
    quarter = rows // splits
    image_emb = jnp.sum(parts.reshape(splits, quarter, embed), axis=0)
    image_unit, image_norm = unit_rows(image_emb)
    low_own = lax.all_gather(image_unit.astype(BF16), "mp", axis=0, tiled=True)
    low_other = swap(low_own, "core")
    positives_other = swap(positives, "core")

    scale = jnp.exp(log_temp[0])
    offset = bias[0]
    at = lax.iota(jnp.int32, count)
    at_ring, at_half, at_row = at // (halves * width), (at // width) % halves, at % width
    at_block = (at_half * rings + at_ring) * cores + core
    column = ((group_id * blocks + at_block) * splits + share) * width + at_row

    def side(low, wanted):
        sims = lax.dot_general(low, piece, (((1,), (1,)), ((), ())), preferred_element_type=F32)
        logits = scale * sims + offset
        signs = jnp.where(column[None, :] == wanted[:, None], 1.0, -1.0).astype(F32)
        loss_sum = -jnp.sum(jax.nn.log_sigmoid(signs * logits))
        slopes = -signs * jax.nn.sigmoid(-signs * logits)
        temp_sum = jnp.sum(slopes * sims)
        bias_sum = jnp.sum(slopes)
        weights = (scale * slopes).astype(BF16)
        return weights, jnp.stack([loss_sum, temp_sum, bias_sum])

    weights_other, sums_other = side(low_other, positives_other)
    grad_other = jnp.dot(weights_other, piece, preferred_element_type=F32)
    grad_other = swap(grad_other, "core")
    weights_own, sums_own = side(low_own, positives)
    grad_own = jnp.dot(weights_own, piece, preferred_element_type=F32)
    sums = sums_own + sums_other

    text_part = lax.dot_general(
        weights_other, low_other, (((0,), (0,)), ((), ())), preferred_element_type=F32
    ) + lax.dot_general(weights_own, low_own, (((0,), (0,)), ((), ())), preferred_element_type=F32)
    text_two = lax.psum_scatter(text_part, "z", scatter_dimension=0, tiled=True)
    text_two = text_two.reshape(halves, width, embed)
    text_keep = lax.dynamic_index_in_dim(text_two, half, 0, keepdims=False)
    text_send = lax.dynamic_index_in_dim(text_two, 1 - half, 0, keepdims=False)
    text_sum = text_keep + swap(text_send, "yh")
    grad_text = unit_backward(text_sum, text_unit, text_norm)

    grad_acc = grad_own + grad_other
    row_part = jnp.sum(low_own.astype(F32) * grad_acc, axis=1)
    strip = embed // groups
    blocks_out = grad_acc.reshape(splits, quarter, groups, strip).transpose(2, 0, 1, 3)
    extra = jnp.concatenate([row_part.reshape(splits, quarter), jnp.zeros((splits, 128 - quarter), F32), jnp.broadcast_to(jnp.pad(sums, (0, strip - 128 - 3)), (splits, strip - 128))], axis=1)
    extra = jnp.broadcast_to(extra[None, :, None, :], (groups, splits, 8, strip))
    sent = jnp.concatenate([blocks_out, extra], axis=2)
    got = lax.all_to_all(sent.reshape(groups * splits, quarter + 8, strip), ("group", "mp"), 0, 0)
    got = jnp.sum(got.reshape(groups * splits, quarter + 8, strip), axis=0)
    row_sum = got[quarter, :quarter]
    sums = got[quarter, 128:131]
    unit_strip = lax.dynamic_slice_in_dim(image_unit, group_id * strip, strip, 1)
    grad_strip = (got[:quarter] - unit_strip * row_sum[:, None]) / image_norm
    low_strip = lax.all_gather(grad_strip.astype(BF16), "mp", axis=0, tiled=True)
    strips = lax.all_gather(low_strip, "group", axis=0, tiled=False)
    grad_image = strips.transpose(1, 0, 2).reshape(rows, embed).astype(F32)

    weight_part = lax.dot_general(
        low_strip, image_hidden, (((0,), (0,)), ((), ())), preferred_element_type=F32
    )
    lanes = -(-(hidden + 3) // 128) * 128
    tail = jnp.broadcast_to(jnp.pad(sums, (0, lanes - hidden - 3)), (strip, lanes - hidden))
    weight_part = jnp.concatenate([weight_part, tail], axis=1)
    places = halves * rings
    own_cols = strip // blocks
    weight_part = weight_part.reshape(places, cores, own_cols, lanes)
    weight_keep = lax.dynamic_index_in_dim(weight_part, core, 1, keepdims=False)
    weight_send = lax.dynamic_index_in_dim(weight_part, 1 - core, 1, keepdims=False)
    weight_part = weight_keep + swap(weight_send, "core")
    weight_got = lax.all_to_all(weight_part, ("yh", "z"), 0, 0)
    weight_sum = jnp.sum(weight_got.reshape(places, own_cols, lanes), axis=0)
    grad_weight = weight_sum[:, :hidden].T
    loss = (weight_sum[0, hidden] / pairs).reshape(1)
    grad_temp = (scale * weight_sum[0, hidden + 1] / pairs).reshape(1)
    grad_bias = (weight_sum[0, hidden + 2] / pairs).reshape(1)
    return (loss, grad_temp, grad_bias, grad_image, grad_text, grad_weight)


def solution(mesh):
    groups, blocks, splits = (mesh.shape[name] for name in ("group", "blk", "mp"))
    fine = Mesh(
        mesh.devices.reshape(groups, 2, blocks // 4, 2, splits),
        ("group", "yh", "z", "core", "mp"),
    )
    blk = ("yh", "z", "core")
    texts = ("group", *blk, "mp")
    in_specs = (P(blk, "mp"), P("mp", None), P(texts, None), P(blk), P(), P())
    out_specs = (P(), P(), P(), P(blk, None), P(texts, None), P("mp", ("group", *blk)))
    return jax.shard_map(
        on_device, mesh=fine, in_specs=in_specs, out_specs=out_specs, check_vma=False
    )
```

```python
import jax
import jax.numpy as jnp
from jax import lax
from jax.sharding import Mesh
from jax.sharding import PartitionSpec as P

F32 = jnp.float32
BF16 = jnp.bfloat16


def unit_rows(values):
    norm_rows = jnp.sqrt(jnp.sum(values * values, axis=1, keepdims=True) + 1e-06)
    return (values / norm_rows, norm_rows)


def unit_backward(grads, unit, norm_rows):
    return (grads - unit * jnp.sum(unit * grads, axis=1, keepdims=True)) / norm_rows


def swap(values, axis):
    return lax.ppermute(values, axis, [(0, 1), (1, 0)])


def shift(values, axes, step):
    size = lax.axis_size(axes)
    return lax.ppermute(values, axes, [(i, (i + step) % size) for i in range(size)])


def exchange(values, axes):
    got = lax.all_to_all(values, axes, 0, 0)
    return got.reshape(values.shape)


def gather(values, axes):
    return exchange(jnp.broadcast_to(values[None], (lax.axis_size(axes), *values.shape)), axes)


RING = ("zs", "zt")
FAR = ("yh", "zs")


def on_device(image_hidden, image_weight, text_embed, positives, log_temp, bias):
    groups = lax.axis_size("group")
    halves = lax.axis_size("yh")
    rings = lax.axis_size(RING)
    turns = lax.axis_size("zt")
    cores = lax.axis_size("core")
    splits = lax.axis_size("mp")
    group_id = lax.axis_index("group")
    turn = lax.axis_index("zt")
    core = lax.axis_index("core")
    share = lax.axis_index("mp")
    rows = image_hidden.shape[0]
    blocks = halves * rings * cores
    pairs = rows * blocks
    width = text_embed.shape[0]
    embed = text_embed.shape[1]
    hidden = image_hidden.shape[1]

    text_unit, text_norm = unit_rows(text_embed.astype(F32))
    text_low = text_unit.astype(BF16)
    with jax.named_scope("text_far"):
        held = gather(text_low, FAR).reshape(-1, embed)
    with jax.named_scope("text_near"):
        after = shift(held, RING, -1)
        before = shift(held, RING, 1)
    piece = jnp.concatenate([held, after, before], axis=0)
    count = piece.shape[0]
    third = held.shape[0]

    image_in, _ = lax.optimization_barrier((image_hidden, text_low))
    quarter = rows // splits

    def partial_for(step):
        place = (share + step) % splits
        chunk = lax.dynamic_slice_in_dim(image_in, place * quarter, quarter, 0)
        return jnp.dot(chunk, image_weight, preferred_element_type=F32)

    with jax.named_scope("image_parts"):
        arrived = [shift(partial_for(step), "mp", step) for step in range(1, splits)]
    image_emb = sum(arrived, partial_for(0))
    image_unit, image_norm = unit_rows(image_emb)
    with jax.named_scope("image_low"):
        lows = gather(image_unit.astype(BF16), ("core", "mp")).reshape(cores, rows, embed)
    low_own = lax.dynamic_index_in_dim(lows, core, 0, keepdims=False)
    low_other = lax.dynamic_index_in_dim(lows, 1 - core, 0, keepdims=False)
    with jax.named_scope("positives"):
        positives_other = swap(positives, "core")

    scale = jnp.exp(log_temp[0])
    offset = bias[0]
    at = lax.iota(jnp.int32, count)
    at_turn = (turn + at // third + jnp.where(at >= 2 * third, turns - 3, 0)) % turns
    at_half, at_step, at_row = at % third // (third // halves), at // width % (rings // turns), at % width
    at_block = (at_half * rings + at_step * turns + at_turn) * cores + core
    column = ((group_id * blocks + at_block) * splits + share) * width + at_row

    def side(low, wanted):
        sims = lax.dot_general(low, piece, (((1,), (1,)), ((), ())), preferred_element_type=F32)
        logits = scale * sims + offset
        signs = jnp.where(column[None, :] == wanted[:, None], 1.0, -1.0).astype(F32)
        losses = -jax.nn.log_sigmoid(signs * logits)
        slopes = -signs * jax.nn.sigmoid(-signs * logits)
        weights = (scale * slopes).astype(BF16)
        return weights, [jnp.sum(v, axis=0) for v in (losses, slopes * sims, slopes)]

    weights_other, sums_other = side(low_other, positives_other)
    grad_other = jnp.dot(weights_other, piece, preferred_element_type=F32)
    low_own, grad_other = lax.optimization_barrier((low_own, grad_other))
    with jax.named_scope("grad_core"):
        grad_other = swap(grad_other, "core")
    weights_own, sums_own = side(low_own, positives)
    grad_own = jnp.dot(weights_own, piece, preferred_element_type=F32)
    weights_other, grad_own = lax.optimization_barrier((weights_other, grad_own))

    text_part = lax.dot_general(
        weights_other, low_other, (((0,), (0,)), ((), ())), preferred_element_type=F32
    ) + lax.dot_general(weights_own, low_own, (((0,), (0,)), ((), ())), preferred_element_type=F32)
    with jax.named_scope("text_back_near"):
        text_held = text_part[:third]
        text_held = text_held + shift(text_part[third : 2 * third], RING, 1)
        text_held = text_held + shift(text_part[2 * third :], RING, -1)

    grad_acc = grad_own + grad_other
    row_part = jnp.sum(low_own.astype(F32) * grad_acc, axis=1)
    strip = embed // groups
    blocks_out = grad_acc.reshape(splits, quarter, groups, strip).transpose(2, 0, 1, 3)
    extra = jnp.zeros((splits, 8, strip), F32)
    extra = extra.at[:, 0, :quarter].set(row_part.reshape(splits, quarter))
    for k in range(3):
        extra = extra.at[:, 1 + k, :count].set((sums_own[k] + sums_other[k])[None])
    extra = jnp.broadcast_to(extra[None], (groups, splits, 8, strip))
    sent = jnp.concatenate([blocks_out, extra], axis=2)
    with jax.named_scope("image_back"):
        got = exchange(sent.reshape(groups * splits, quarter + 8, strip), ("group", "mp"))
    text_held, got = lax.optimization_barrier((text_held, got))
    with jax.named_scope("text_back_far"):
        text_got = exchange(text_held.reshape(-1, width, embed), FAR)
    got = jnp.sum(got, axis=0)
    row_sum = got[quarter, :quarter]
    sums = jnp.sum(got[quarter + 1 : quarter + 4], axis=1)
    unit_strip = lax.dynamic_slice_in_dim(image_unit, group_id * strip, strip, 1)
    grad_strip = (got[:quarter] - unit_strip * row_sum[:, None]) / image_norm
    with jax.named_scope("strip_mp"):
        low_strip = lax.all_gather(grad_strip.astype(BF16), "mp", axis=0, tiled=True)
    with jax.named_scope("strip_group"):
        grad_image = jnp.zeros((rows, embed), F32)
        for step in range(groups):
            strip_from = shift(low_strip, "group", step) if step else low_strip
            place = (group_id - step) % groups * strip
            grad_image = lax.dynamic_update_slice_in_dim(grad_image, strip_from.astype(F32), place, 1)

    weight_part = lax.dot_general(
        low_strip, image_hidden, (((0,), (0,)), ((), ())), preferred_element_type=F32
    )
    lanes = -(-(hidden + 3) // 128) * 128
    tail = jnp.broadcast_to(jnp.pad(sums, (0, lanes - hidden - 3)), (strip, lanes - hidden))
    weight_part = jnp.concatenate([weight_part, tail], axis=1)
    places = halves * rings
    own_cols = strip // blocks
    weight_part = weight_part.reshape(places, cores, own_cols, lanes)
    weight_keep = lax.dynamic_index_in_dim(weight_part, core, 1, keepdims=False)
    weight_send = lax.dynamic_index_in_dim(weight_part, 1 - core, 1, keepdims=False)
    with jax.named_scope("weight_core"):
        weight_part = weight_keep + swap(weight_send, "core")
    weight_part, text_got = lax.optimization_barrier((weight_part, text_got))
    grad_text = unit_backward(jnp.sum(text_got, axis=0), text_unit, text_norm)
    with jax.named_scope("weight_far"):
        weight_sum = jnp.sum(exchange(weight_part, ("yh", *RING)), axis=0)
    grad_weight = weight_sum[:, :hidden].T
    loss = (weight_sum[0, hidden] / pairs).reshape(1)
    grad_temp = (scale * weight_sum[0, hidden + 1] / pairs).reshape(1)
    grad_bias = (weight_sum[0, hidden + 2] / pairs).reshape(1)
    return (loss, grad_temp, grad_bias, grad_image, grad_text, grad_weight)


def solution(mesh):
    groups, blocks, splits = (mesh.shape[name] for name in ("group", "blk", "mp"))
    fine = Mesh(
        mesh.devices.reshape(groups, 2, blocks // 12, 3, 2, splits),
        ("group", "yh", "zs", "zt", "core", "mp"),
    )
    blk = ("yh", "zs", "zt", "core")
    texts = ("group", *blk, "mp")
    in_specs = (P(blk, "mp"), P("mp", None), P(texts, None), P(blk), P(), P())
    out_specs = (P(), P(), P(), P(blk, None), P(texts, None), P("mp", ("group", *blk)))
    return jax.shard_map(
        on_device, mesh=fine, in_specs=in_specs, out_specs=out_specs, check_vma=False
    )
```

```python
import functools

import jax
import jax.numpy as jnp
from jax import lax
from jax.experimental import pallas as pl
from jax.experimental.pallas import tpu as pltpu
from jax.sharding import Mesh
from jax.sharding import PartitionSpec as P


F32 = jnp.float32
BF16 = jnp.bfloat16


def unit_rows(values):
    norm_rows = jnp.sqrt(jnp.sum(values * values, axis=1, keepdims=True) + 1e-06)
    return (values / norm_rows, norm_rows)


def unit_backward(grads, unit, norm_rows):
    return (grads - unit * jnp.sum(unit * grads, axis=1, keepdims=True)) / norm_rows


def swap(values, axis):
    return lax.ppermute(values, axis, [(0, 1), (1, 0)])


def shift(values, axes, step):
    size = lax.axis_size(axes)
    return lax.ppermute(values, axes, [(i, (i + step) % size) for i in range(size)])


def exchange(values, axes):
    got = lax.all_to_all(values, axes, 0, 0)
    return got.reshape(values.shape)


def gather(values, axes):
    return exchange(jnp.broadcast_to(values[None], (lax.axis_size(axes), *values.shape)), axes)


NT = (((1,), (1,)), ((), ()))


def side_kernel(sizes, factors, ids, low, held, after, before, wanted, earlier, weights, sent, totals):
    groups, splits, quarter, strip, halves, rings, turns, cores, width = sizes
    scale, offset = factors[0], factors[1]
    group_id, turn, core, share = ids[0], ids[1], ids[2], ids[3]
    blocks = halves * rings * cores
    third = held.shape[0]
    rows = low.shape[0]
    low_rows = low[...]
    wanted_row = wanted[...]
    grads = jnp.zeros((rows, low.shape[1]), F32)
    row_part = jnp.zeros((1, rows), F32)
    sums = [jnp.zeros((1, rows), F32)] * 3
    for k, piece in enumerate((held, after, before)):
        texts = piece[...]
        at = lax.broadcasted_iota(jnp.int32, (third, rows), 0)
        at_turn = lax.rem(turn + (0, 1, turns - 1)[k], turns)
        steps = rings // turns
        at_place = at // width
        at_block = ((at_place // steps) * rings + (at_place % steps) * turns + at_turn) * cores + core
        column = ((group_id * blocks + at_block) * splits + share) * width + at % width
        sims = lax.dot_general(texts, low_rows, NT, preferred_element_type=F32)
        logits = scale * sims + offset
        signs = jnp.where(column == wanted_row, 1.0, -1.0).astype(F32)
        x = -signs * logits
        small = jnp.exp(-jnp.abs(x))
        losses = jnp.maximum(x, 0.0) + jnp.log1p(small)
        slopes = -signs * (jnp.where(x >= 0, 1.0, small) / (1.0 + small))
        value = (scale * slopes).astype(BF16)
        weights[k * third : (k + 1) * third, :] = value
        value = value.astype(F32)
        grads = grads + lax.dot_general(
            value.T.astype(BF16), texts, (((1,), (0,)), ((), ())), preferred_element_type=F32
        )
        row_part = row_part + jnp.sum(value * sims, axis=0, keepdims=True)
        for i, v in enumerate((losses, slopes * sims, slopes)):
            sums[i] = sums[i] + jnp.sum(v, axis=0, keepdims=True)
    sums = jnp.concatenate(sums, axis=0) + earlier[0:3, :]
    totals[...] = jnp.concatenate([sums, jnp.zeros((5, rows), F32)], axis=0)
    low_wide = low_rows.astype(F32)
    grads = grads - low_wide * jnp.sum(low_wide * grads, axis=1, keepdims=True)
    lines = [row_part]
    if sent.dtype == F32:
        for k in range(3):
            high = sums[k : k + 1].astype(BF16).astype(F32)
            lines += [high, sums[k : k + 1] - high]
    more = jnp.concatenate([*lines, jnp.zeros((16 - len(lines), rows), F32)], axis=0)
    if strip > rows:
        more = jnp.concatenate([more, jnp.zeros((16, strip - rows), F32)], axis=1)
    for g in range(groups):
        for m in range(splits):
            block = grads[m * quarter : (m + 1) * quarter, g * strip : (g + 1) * strip]
            sent[g * splits + m, :quarter, :] = block.astype(sent.dtype)
            sent[g * splits + m, quarter:, :] = more.astype(sent.dtype)


def text_kernel(weights_own, low_own, weights_other, low_other, held, after, before, *outs):
    third, embed = held.shape
    for k, (piece, out) in enumerate(zip((held, after, before), outs)):
        at = slice(k * third, (k + 1) * third)
        grads = jnp.dot(
            weights_own[at, :], low_own[...], preferred_element_type=F32
        ) + jnp.dot(weights_other[at, :], low_other[...], preferred_element_type=F32)
        texts = piece[...].astype(F32)
        row_part = jnp.sum(texts * grads, axis=1, keepdims=True)
        out[:, :embed] = (grads - texts * row_part).astype(out.dtype)
        out[:, embed:] = jnp.broadcast_to(row_part, (third, 128)).astype(out.dtype)


RING = ("zs", "zt")
FAR = ("yh", "zs")


def on_device(image_hidden, image_weight, text_embed, positives, log_temp, bias):
    groups = lax.axis_size("group")
    halves = lax.axis_size("yh")
    rings = lax.axis_size(RING)
    turns = lax.axis_size("zt")
    cores = lax.axis_size("core")
    splits = lax.axis_size("mp")
    group_id = lax.axis_index("group")
    turn = lax.axis_index("zt")
    core = lax.axis_index("core")
    share = lax.axis_index("mp")
    rows = image_hidden.shape[0]
    blocks = halves * rings * cores
    pairs = rows * blocks
    width = text_embed.shape[0]
    embed = text_embed.shape[1]
    hidden = image_hidden.shape[1]

    text_unit, text_norm = unit_rows(text_embed.astype(F32))
    text_low = text_unit.astype(BF16)
    held = gather(text_low, FAR).reshape(-1, embed)
    after = shift(held, RING, -1)
    before = shift(held, RING, 1)
    third = held.shape[0]

    quarter = rows // splits

    def partial_for(step):
        place = (share + step) % splits
        chunk = lax.dynamic_slice_in_dim(image_hidden, place * quarter, quarter, 0)
        return jnp.dot(chunk, image_weight, preferred_element_type=F32)

    arrived = [shift(partial_for(step), "mp", step) for step in range(1, splits)]
    image_emb = sum(arrived, partial_for(0))
    image_unit, image_norm = unit_rows(image_emb)
    image_low = image_unit.astype(BF16)
    low_own = lax.all_gather(image_low, "mp", axis=0, tiled=True)
    low_other = swap(low_own, "core")
    positives_other = swap(positives, "core")

    scale = jnp.exp(log_temp[0])
    strip = embed // groups
    factors = jnp.concatenate([jnp.exp(log_temp), bias])
    ids = jnp.stack([group_id, turn, core, share]).astype(jnp.int32)
    sizes = (groups, splits, quarter, strip, halves, rings, turns, cores, width)
    smem = pl.BlockSpec(memory_space=pltpu.SMEM)
    vmem = pl.BlockSpec(memory_space=pltpu.VMEM)

    def side(low, wanted, earlier, kind):
        return pl.pallas_call(
            functools.partial(side_kernel, sizes),
            out_shape=(
                jax.ShapeDtypeStruct((3 * third, rows), BF16),
                jax.ShapeDtypeStruct((groups * splits, quarter + 16, strip), kind),
                jax.ShapeDtypeStruct((8, rows), F32),
            ),
            in_specs=[smem, smem, vmem, vmem, vmem, vmem, vmem, vmem],
            out_specs=(vmem, vmem, vmem),
            name="side",
        )(factors, ids, low, held, after, before, wanted.reshape(1, rows), earlier)

    weights_other, sent_other, totals = side(
        low_other, positives_other, jnp.zeros((8, rows), F32), BF16
    )
    sent_other = swap(sent_other, "core")
    weights_own, sent_own, _ = side(low_own, positives, totals, F32)
    sent = (sent_own + sent_other.astype(F32)).astype(BF16)
    weights_other, sent = lax.optimization_barrier((weights_other, sent))

    text_held, text_after, text_before = pl.pallas_call(
        text_kernel,
        out_shape=tuple(jax.ShapeDtypeStruct((third, embed + 128), k) for k in (F32, BF16, BF16)),
        in_specs=[vmem] * 7,
        out_specs=(vmem,) * 3,
        name="text_part",
    )(weights_own, low_own, weights_other, low_other, held, after, before)
    text_after = shift(text_after, RING, 1).astype(F32)
    text_before = shift(text_before, RING, -1).astype(F32)
    text_held = (text_held + text_after + text_before).astype(BF16)

    got = exchange(sent, ("group", "mp"))
    text_held, got = lax.optimization_barrier((text_held, got))
    text_got = exchange(text_held.reshape(-1, width, embed + 128), FAR)
    got = jnp.sum(got.astype(F32), axis=0)
    row_sum = lax.dynamic_slice_in_dim(got[quarter], share * quarter, quarter, 0)
    sums = jnp.sum(got[quarter + 1 : quarter + 7].reshape(3, 2 * strip), axis=1)
    unit_strip = lax.dynamic_slice_in_dim(image_unit, group_id * strip, strip, 1)
    off = unit_strip.astype(BF16).astype(F32) - unit_strip
    grad_strip = (got[:quarter] + off * row_sum[:, None]) / image_norm
    low_strip = lax.all_gather(grad_strip.astype(BF16), "mp", axis=0, tiled=True)
    grad_image = jnp.zeros((rows, embed), F32)
    for step in range(groups):
        strip_from = shift(low_strip, "group", step) if step else low_strip
        place = (group_id - step) % groups * strip
        grad_image = lax.dynamic_update_slice_in_dim(grad_image, strip_from.astype(F32), place, 1)

    weight_part = lax.dot_general(
        low_strip, image_hidden, (((0,), (0,)), ((), ())), preferred_element_type=F32
    )
    lanes = -(-(hidden + 3) // 128) * 128
    tail = jnp.broadcast_to(jnp.pad(sums, (0, lanes - hidden - 3)), (strip, lanes - hidden))
    weight_part = jnp.concatenate([weight_part, tail], axis=1)
    places = halves * rings
    own_cols = strip // blocks
    weight_part = weight_part.reshape(places, cores, own_cols, lanes)
    weight_keep = lax.dynamic_index_in_dim(weight_part, core, 1, keepdims=False)
    weight_send = lax.dynamic_index_in_dim(weight_part, 1 - core, 1, keepdims=False)
    weight_part = weight_keep + swap(weight_send, "core")
    weight_part, text_got = lax.optimization_barrier((weight_part, text_got))
    text_got = jnp.sum(text_got.astype(F32), axis=0)
    text_sum = text_got[:, :embed] + text_low.astype(F32) * text_got[:, embed : embed + 1]
    grad_text = unit_backward(text_sum, text_unit, text_norm)
    weight_sum = jnp.sum(exchange(weight_part, ("yh", *RING)), axis=0)
    grad_weight = weight_sum[:, :hidden].T
    loss = (weight_sum[0, hidden] / pairs).reshape(1)
    grad_temp = (scale * weight_sum[0, hidden + 1] / pairs).reshape(1)
    grad_bias = (weight_sum[0, hidden + 2] / pairs).reshape(1)
    return (loss, grad_temp, grad_bias, grad_image, grad_text, grad_weight)


def solution(mesh):
    groups, blocks, splits = (mesh.shape[name] for name in ("group", "blk", "mp"))
    fine = Mesh(
        mesh.devices.reshape(groups, 2, blocks // 12, 3, 2, splits),
        ("group", "yh", "zs", "zt", "core", "mp"),
    )
    blk = ("yh", "zs", "zt", "core")
    texts = ("group", *blk, "mp")
    in_specs = (P(blk, "mp"), P("mp", None), P(texts, None), P(blk), P(), P())
    out_specs = (P(), P(), P(), P(blk, None), P(texts, None), P("mp", ("group", *blk)))
    return jax.shard_map(
        on_device, mesh=fine, in_specs=in_specs, out_specs=out_specs, check_vma=False
    )
```
